256 devices in a mesh: expert: 64 (over x, z, core), replica: 4 (over y).
Axes of the slice: x: 4, y: 4, z: 8, core: 2. Of those that a mesh axis runs over, the one named last changes fastest.
Arguments:
- tokens: bfloat16 [16384, 2048], P(('expert', 'replica')), may hold values from -6 to 6
- route_ids: int32 [16384, 6], P(('expert', 'replica')), may hold values from 0 to 63, all different within a row; in each aligned block of 64 rows (0 to 63, 64 to 127, ...) at most 8 rows name the same one
- gate_probs: float32 [16384, 6], P(('expert', 'replica')), may hold values from 0.05 to 0.35
- out_cot: bfloat16 [16384, 2048], P(('expert', 'replica')), may hold values from -6 to 6
- w_gate: bfloat16 [64, 2048, 768], P('expert'), may hold values from -0.125 to 0.125
- w_up: bfloat16 [64, 2048, 768], P('expert'), may hold values from -0.125 to 0.125
- w_down: bfloat16 [64, 768, 2048], P('expert'), may hold values from -0.21875 to 0.21875
Outputs:
- combined: bfloat16 [16384, 2048], P(('expert', 'replica'))
- grad_tokens: bfloat16 [16384, 2048], P(('expert', 'replica'))
- grad_gate: bfloat16 [64, 2048, 768], P('expert', 'replica')
- grad_up: bfloat16 [64, 2048, 768], P('expert', 'replica')
- grad_down: bfloat16 [64, 768, 2048], P('expert', 'replica')
The draws below stay inside these ranges and needn't reach their ends.
Inputs may be any that keep to these rules, and one draw needn't show every extreme that they name: `route_ids`: A token's 6 experts differ. Among the 64 tokens of one device, at most 8 choose any one expert, and in every draw some device's tokens choose some expert exactly 8 times.
All inputs are finite; a program needn't handle non-finite values.
Results may differ from the reference program's by a relative error of at most 0.0095.
Values may be sent and summed in bfloat16 or wider, within the bound.
A program may use at most 128 MiB of HBM per device.

```python
import math
import jax
import jax.numpy as jnp
import numpy as np
from jax import lax

D = 2048
H = 768
TOPK = 6
TOK_DEV = 64
EXPERTS = 64
CAP = 8
TOKENS = 16384
N_EXPERT = 64
N_REPLICA = 4


def block_levels(rng, dims, shards, low, largest):
    gain, own = 1.0, jax.random.fold_in(rng, 6)
    for position, shards_of in shards:
        draws = jnp.exp(jax.random.uniform(jax.random.fold_in(own, position), (shards_of,), jnp.float32, low / len(shards), largest / len(shards)))
        gain = gain * jnp.repeat(draws, dims[position] // shards_of).reshape([-1 if axis == position else 1 for axis in range(len(dims))])
    return gain


def routed_block(rng, own, number, rows, number_of, top, most, slope):
    ranking = jax.random.permutation(rng, number_of)
    heavy_load, usual = load_shares(number_of, rows * top, most, slope, True), load_shares(number_of, rows * top, most, slope, False)
    places = jnp.arange(number_of)

    def named(sizes, rotation):
        used = int((sizes > 0).sum())
        fixed = max(1, used // 4)
        shifted = fixed + (places - fixed + rotation * (used - fixed)) % max(1, number_of - fixed)
        return jnp.zeros((number_of,), jnp.int32).at[ranking[jnp.where(places < fixed, places, shifted)]].set(jnp.asarray(sizes, jnp.int32))

    sizes = jnp.where(number % 4 == 0, named(heavy_load, number // 4), named(usual, number - number // 4 - 1))
    mixed = jax.random.permutation(jax.random.fold_in(own, 3), number_of)
    giver, receiver = mixed[0:number_of // 2 * 2:2], mixed[1:number_of // 2 * 2:2]
    room = jnp.minimum(sizes[giver] - 1, most - sizes[receiver]) // 2
    room = jnp.where((giver == ranking[0]) | (receiver == ranking[0]) | (sizes[receiver] == 0), 0, jnp.maximum(room, 0))
    shifted = jax.random.randint(jax.random.fold_in(own, 4), (number_of // 2,), 0, 1 << 20) % (room + 1)
    sizes = sizes.at[giver].add(-shifted).at[receiver].add(shifted)
    members = jnp.searchsorted(jnp.cumsum(sizes), jnp.arange(rows * top), side="right").astype(jnp.int32)
    listing = members.reshape(top, rows).T
    listing = listing[jax.random.permutation(jax.random.fold_in(own, 1), rows)]
    rotation = jax.random.randint(jax.random.fold_in(own, 2), (rows, 1), 0, top)
    return jnp.take_along_axis(listing, (jnp.arange(top)[None, :] + rotation) % top, axis=1)


def load_shares(amount, total, most, skew, full):
    portions = [(1 << 20) // math.isqrt(rank ** skew) + 1 for rank in range(1, amount + 1)]
    largest = most if full else min(most, max(-(-total // amount), total * portions[0] // sum(portions)))
    least = 1 if total - largest >= amount - 1 else 0
    holding, spare = [largest] + [least] * (amount - 1), total - largest - least * (amount - 1)
    while spare > 0:
        free = [i for i in range(1, amount) if holding[i] < largest] or [i for i in range(1, amount) if holding[i] < most]
        mass, left = sum([portions[i] for i in free]), spare
        for i in free:
            more = min(most - holding[i], max(1, left * portions[i] // mass), spare)
            holding[i] = holding[i] + more
            spare = spare - more
    return np.array(holding)


def bell_draw(key, shape, spread, reach, split=(), kind=jnp.bfloat16):
    values = jax.random.normal(key, shape, jnp.float32) * spread
    if len(split) > 0:
        values = block_levels(key, shape, split, -0.22, 0.18) * values
    return jnp.clip(values, min=-reach, max=reach).astype(kind)


def setup_inputs(seed: int = 0) -> dict:
    seeds = jax.random.split(jax.random.key(seed), 8)
    tokens = bell_draw(seeds[0], (TOKENS, D), 1.0, 6.0, ((0, 256),))
    route_ids_keys = jax.random.split(jax.random.fold_in(seeds[1], 1), TOKENS // TOK_DEV)
    route_ids_turns = jax.random.permutation(jax.random.fold_in(seeds[1], 3), TOKENS // TOK_DEV)
    route_ids = jax.vmap(lambda own, number: routed_block(jax.random.fold_in(seeds[1], 2), own, number, TOK_DEV, EXPERTS, TOPK, CAP, 2))(route_ids_keys, route_ids_turns).reshape((TOKENS, TOPK))
    gate_probs = jnp.clip(0.05 + 0.29999999 * jax.random.uniform(seeds[2], (TOKENS, TOPK), jnp.float32) ** block_levels(seeds[2], (TOKENS, TOPK), ((0, 256),), -0.2, 0.2), 0.05, 0.35)
    out_cot = bell_draw(seeds[3], (TOKENS, D), 1.0, 6.0, ((0, 256),))
    w_gate = bell_draw(seeds[4], (EXPERTS, D, H), D ** -0.5, 0.125, ((0, 64),))
    w_up = bell_draw(seeds[5], (EXPERTS, D, H), D ** -0.5, 0.125, ((0, 64),))
    w_down = bell_draw(seeds[6], (EXPERTS, H, D), H ** -0.5, 0.21875, ((0, 64),))
    return dict(tokens=tokens, route_ids=route_ids, gate_probs=gate_probs, out_cot=out_cot, w_gate=w_gate, w_up=w_up, w_down=w_down)


def slots(routes, experts, capacity):
    flat_ids = routes.reshape(-1).astype(jnp.int32)
    one_hot = (flat_ids[:, None] == jnp.arange(experts, dtype=jnp.int32)[None, :]).astype(jnp.int32)
    before = jnp.cumsum(one_hot, axis=0) - one_hot
    slot_rank = jnp.sum(before * one_hot, axis=1)
    return (flat_ids * capacity + slot_rank).astype(jnp.int32)


def place(token_rows, positions, total_rows):
    return jnp.zeros((total_rows, token_rows.shape[1]), token_rows.dtype).at[positions].set(token_rows)


def hidden_rows(token_rows, gate_weight, up_weight):
    pre_gate = jnp.dot(token_rows, gate_weight, preferred_element_type=jnp.float32)
    pre_up = jnp.dot(token_rows, up_weight, preferred_element_type=jnp.float32)
    activation = (jax.nn.silu(pre_gate) * pre_up).astype(jnp.bfloat16)
    return pre_gate, pre_up, activation


def backward_rows(grad_rows, pre_gate, pre_up, gate_weight, up_weight, down_weight):
    contract = (((1,), (1,)), ((), ()))
    d_hidden = lax.dot_general(grad_rows, down_weight, contract, preferred_element_type=jnp.float32)
    sigmoid_gate = jax.nn.sigmoid(pre_gate)
    d_gate = (d_hidden * pre_up * sigmoid_gate * (1.0 + pre_gate * (1.0 - sigmoid_gate))).astype(jnp.bfloat16)
    d_up = (d_hidden * pre_gate * sigmoid_gate).astype(jnp.bfloat16)
    back_rows = lax.dot_general(d_gate, gate_weight, contract, preferred_element_type=jnp.float32)
    back_rows = back_rows + lax.dot_general(d_up, up_weight, contract, preferred_element_type=jnp.float32)
    return back_rows.astype(jnp.bfloat16), d_gate, d_up


def outer_sum(left, right):
    return lax.dot_general(left, right, (((0,), (0,)), ((), ())), preferred_element_type=jnp.float32)


def reference(tokens, route_ids, gate_probs, out_cot, w_gate, w_up, w_down):
    owners = N_EXPERT
    groups = N_REPLICA
    total_rows = EXPERTS * CAP

    def slots_one(routes):
        return slots(routes, EXPERTS, CAP)

    def place_one(token_rows, positions):
        return place(token_rows, positions, total_rows)

    def pick_one(table, positions):
        return table[positions]

    positions = jax.vmap(jax.vmap(slots_one))(route_ids.reshape(owners, groups, TOK_DEV, TOPK))
    token_rows = jnp.repeat(tokens.reshape(owners, groups, TOK_DEV, D), TOPK, axis=2)
    shares = gate_probs.reshape(owners, groups, TOK_DEV, TOPK)
    cotangent = out_cot.reshape(owners, groups, TOK_DEV, D).astype(jnp.float32)
    scaled = (shares[..., None] * cotangent[:, :, :, None, :]).astype(jnp.bfloat16)
    scaled = scaled.reshape(owners, groups, TOK_DEV * TOPK, D)
    outgoing = jax.vmap(jax.vmap(place_one))(token_rows, positions).reshape(owners, groups, EXPERTS, CAP, D)
    grad_out = jax.vmap(jax.vmap(place_one))(scaled, positions).reshape(owners, groups, EXPERTS, CAP, D)
    received = jnp.transpose(outgoing, (2, 1, 0, 3, 4)).reshape(EXPERTS, groups, owners * CAP, D)
    grads_in = jnp.transpose(grad_out, (2, 1, 0, 3, 4)).reshape(EXPERTS, groups, owners * CAP, D)

    def one_expert(operands):
        rows_e, grads_e, gate_weight, up_weight, down_weight = operands

        def one_group(rows_g, grads_g):
            pre_gate, pre_up, activation = hidden_rows(rows_g, gate_weight, up_weight)
            result = jnp.dot(activation, down_weight, preferred_element_type=jnp.float32).astype(jnp.bfloat16)
            back_rows, d_gate, d_up = backward_rows(grads_g, pre_gate, pre_up, gate_weight, up_weight, down_weight)
            part_gate = outer_sum(rows_g, d_gate).astype(jnp.bfloat16)
            part_up = outer_sum(rows_g, d_up).astype(jnp.bfloat16)
            part_down = outer_sum(activation, grads_g).astype(jnp.bfloat16)
            return result, back_rows, part_gate, part_up, part_down

        result, back_rows, part_gate, part_up, part_down = jax.vmap(one_group)(rows_e, grads_e)
        part_gate, part_up, part_down = lax.optimization_barrier((part_gate, part_up, part_down))
        sum_gate = jnp.sum(part_gate.astype(jnp.float32), axis=0).astype(jnp.bfloat16)
        sum_up = jnp.sum(part_up.astype(jnp.float32), axis=0).astype(jnp.bfloat16)
        sum_down = jnp.sum(part_down.astype(jnp.float32), axis=0).astype(jnp.bfloat16)
        return result, back_rows, sum_gate, sum_up, sum_down

    results, backs, grad_gate, grad_up, grad_down = lax.map(one_expert, (received, grads_in, w_gate, w_up, w_down))
    results = jnp.transpose(results.reshape(EXPERTS, groups, owners, CAP, D), (2, 1, 0, 3, 4)).reshape(owners, groups, total_rows, D)
    backs = jnp.transpose(backs.reshape(EXPERTS, groups, owners, CAP, D), (2, 1, 0, 3, 4)).reshape(owners, groups, total_rows, D)
    picked = jax.vmap(jax.vmap(pick_one))(results, positions).reshape(owners, groups, TOK_DEV, TOPK, D)
    combined = jnp.sum(shares[..., None] * picked.astype(jnp.float32), axis=3).astype(jnp.bfloat16)
    picked_grad = jax.vmap(jax.vmap(pick_one))(backs, positions).reshape(owners, groups, TOK_DEV, TOPK, D)
    grad_tokens = jnp.sum(picked_grad.astype(jnp.float32), axis=3).astype(jnp.bfloat16)
    return (combined.reshape(TOKENS, D), grad_tokens.reshape(TOKENS, D), grad_gate, grad_up, grad_down)
```

```python
import jax
import jax.numpy as jnp
from jax import lax
from jax.sharding import PartitionSpec as P


def slots(routes, experts, capacity):
    flat_ids = routes.reshape(-1)
    one_hot = (flat_ids[:, None] == jnp.arange(experts, dtype=jnp.int32)[None, :]).astype(jnp.int32)
    before = jnp.cumsum(one_hot, axis=0) - one_hot
    slot_rank = jnp.sum(before * one_hot, axis=1)
    return flat_ids * capacity + slot_rank


def hidden_rows(token_rows, gate_weight, up_weight):
    pre_gate = jnp.dot(token_rows, gate_weight, preferred_element_type=jnp.float32)
    pre_up = jnp.dot(token_rows, up_weight, preferred_element_type=jnp.float32)
    activation = (jax.nn.silu(pre_gate) * pre_up).astype(jnp.bfloat16)
    return (pre_gate, pre_up, activation)


def backward_rows(grad_rows, pre_gate, pre_up, gate_weight, up_weight, down_weight):
    contract = (((1,), (1,)), ((), ()))
    d_hidden = lax.dot_general(grad_rows, down_weight, contract, preferred_element_type=jnp.float32)
    sigmoid_gate = jax.nn.sigmoid(pre_gate)
    d_gate = (d_hidden * pre_up * sigmoid_gate * (1.0 + pre_gate * (1.0 - sigmoid_gate))).astype(
        jnp.bfloat16
    )
    d_up = (d_hidden * pre_gate * sigmoid_gate).astype(jnp.bfloat16)
    back_rows = lax.dot_general(d_gate, gate_weight, contract, preferred_element_type=jnp.float32)
    back_rows = back_rows + lax.dot_general(
        d_up, up_weight, contract, preferred_element_type=jnp.float32
    )
    return (back_rows.astype(jnp.bfloat16), d_gate, d_up)


def outer_sum(left, right):
    return lax.dot_general(
        left, right, (((0,), (0,)), ((), ())), preferred_element_type=jnp.float32
    )


def exchange(blocks):
    return lax.all_to_all(blocks, "expert", split_axis=0, concat_axis=0, tiled=True)


def per_device(tokens, route_ids, gate_probs, out_cot, w_gate, w_up, w_down):
    experts = lax.axis_size("expert")
    tok_rows, features = tokens.shape
    top_count = route_ids.shape[1]
    hidden = w_gate.shape[2]
    capacity = max(2, tok_rows * top_count * 4 // (3 * experts))
    total_rows = experts * capacity
    positions = slots(route_ids, experts, capacity)
    gate_weight = w_gate[0]
    up_weight = w_up[0]
    down_weight = w_down[0]
    pick = (positions[:, None] == jnp.arange(total_rows, dtype=positions.dtype)[None, :]).astype(
        jnp.bfloat16
    )
    pick3 = pick.reshape(tok_rows, top_count, total_rows)
    owner = jnp.sum(pick3, axis=1)
    outgoing = jnp.dot(owner.T, tokens, preferred_element_type=jnp.float32).astype(jnp.bfloat16)
    slot_rows = exchange(outgoing.reshape(experts, capacity, features)).reshape(-1, features)
    scaled = (gate_probs[:, :, None] * out_cot[:, None, :].astype(jnp.float32)).astype(jnp.bfloat16)
    grad_out = jnp.dot(
        pick.T, scaled.reshape(-1, features), preferred_element_type=jnp.float32
    ).astype(jnp.bfloat16)
    grads_in = exchange(grad_out.reshape(experts, capacity, features)).reshape(-1, features)

    pre_gate, pre_up, activation = hidden_rows(slot_rows, gate_weight, up_weight)
    result = jnp.dot(activation, down_weight, preferred_element_type=jnp.float32).astype(
        jnp.bfloat16
    )
    returned = exchange(result.reshape(experts, capacity, features)).reshape(-1, features)
    back_rows, d_gate, d_up = backward_rows(
        grads_in, pre_gate, pre_up, gate_weight, up_weight, down_weight
    )
    returned_grad = exchange(back_rows.reshape(experts, capacity, features)).reshape(-1, features)

    picked = jnp.einsum("tkp,pd->tkd", pick3, returned, preferred_element_type=jnp.float32)
    combined = jnp.einsum("tk,tkd->td", gate_probs, picked).astype(jnp.bfloat16)
    grad_tokens = jnp.dot(owner, returned_grad, preferred_element_type=jnp.float32).astype(
        jnp.bfloat16
    )

    gate_up_grad = jnp.concatenate([d_gate, d_up], axis=1)
    gate_up_sum = lax.psum_scatter(
        outer_sum(slot_rows, gate_up_grad).astype(jnp.bfloat16),
        "replica",
        scatter_dimension=0,
        tiled=True,
    ).astype(jnp.float32)
    down_sum = lax.psum_scatter(
        outer_sum(activation, grads_in).astype(jnp.bfloat16),
        "replica",
        scatter_dimension=0,
        tiled=True,
    )
    grad_gate = gate_up_sum[:, :hidden].astype(jnp.bfloat16)[None]
    grad_up = gate_up_sum[:, hidden:].astype(jnp.bfloat16)[None]
    grad_down = down_sum[None]
    return (combined, grad_tokens, grad_gate, grad_up, grad_down)


def solution(mesh):
    placed = (
        P(("expert", "replica"), None),
        P(("expert", "replica"), None),
        P(("expert", "replica"), None),
        P(("expert", "replica"), None),
        P("expert", None, None),
        P("expert", None, None),
        P("expert", None, None),
    )
    return jax.shard_map(
        per_device,
        mesh=mesh,
        in_specs=placed,
        out_specs=(
            P(("expert", "replica"), None),
            P(("expert", "replica"), None),
            P("expert", "replica", None),
            P("expert", "replica", None),
            P("expert", "replica", None),
        ),
        check_vma=False,
    )
```

```python
import jax
import jax.numpy as jnp
from jax import lax
from jax.sharding import PartitionSpec as P


def slots(routes, experts, capacity):
    flat_ids = routes.reshape(-1)
    one_hot = (flat_ids[:, None] == jnp.arange(experts, dtype=jnp.int32)[None, :]).astype(jnp.int32)
    before = jnp.cumsum(one_hot, axis=0) - one_hot
    slot_rank = jnp.sum(before * one_hot, axis=1)
    return flat_ids * capacity + slot_rank


def hidden_rows(token_rows, gate_weight, up_weight):
    pre_gate = jnp.dot(token_rows, gate_weight, preferred_element_type=jnp.float32)
    pre_up = jnp.dot(token_rows, up_weight, preferred_element_type=jnp.float32)
    activation = (jax.nn.silu(pre_gate) * pre_up).astype(jnp.bfloat16)
    return (pre_gate, pre_up, activation)


def backward_rows(grad_rows, pre_gate, pre_up, gate_weight, up_weight, down_weight):
    contract = (((1,), (1,)), ((), ()))
    d_hidden = lax.dot_general(grad_rows, down_weight, contract, preferred_element_type=jnp.float32)
    sigmoid_gate = jax.nn.sigmoid(pre_gate)
    d_gate = (d_hidden * pre_up * sigmoid_gate * (1.0 + pre_gate * (1.0 - sigmoid_gate))).astype(
        jnp.bfloat16
    )
    d_up = (d_hidden * pre_gate * sigmoid_gate).astype(jnp.bfloat16)
    back_rows = lax.dot_general(d_gate, gate_weight, contract, preferred_element_type=jnp.float32)
    back_rows = back_rows + lax.dot_general(
        d_up, up_weight, contract, preferred_element_type=jnp.float32
    )
    return (back_rows.astype(jnp.bfloat16), d_gate, d_up)


def outer_sum(left, right):
    return lax.dot_general(
        left, right, (((0,), (0,)), ((), ())), preferred_element_type=jnp.float32
    )


def exchange(blocks):
    return lax.all_to_all(blocks, "expert", split_axis=0, concat_axis=0, tiled=True)


def per_device(tokens, route_ids, gate_probs, out_cot, w_gate, w_up, w_down):
    experts = lax.axis_size("expert")
    tok_rows, features = tokens.shape
    top_count = route_ids.shape[1]
    hidden = w_gate.shape[2]
    capacity = max(2, tok_rows * top_count * 4 // (3 * experts))
    total_rows = experts * capacity
    positions = slots(route_ids, experts, capacity)
    gate_weight = w_gate[0]
    up_weight = w_up[0]
    down_weight = w_down[0]
    pick = (positions[:, None] == jnp.arange(total_rows, dtype=positions.dtype)[None, :]).astype(
        jnp.bfloat16
    )
    pick3 = pick.reshape(tok_rows, top_count, total_rows)
    owner = jnp.sum(pick3, axis=1)
    outgoing = jnp.dot(owner.T, tokens, preferred_element_type=jnp.float32).astype(jnp.bfloat16)
    slot_rows = exchange(outgoing.reshape(experts, capacity, features)).reshape(-1, features)
    scaled = (gate_probs[:, :, None] * out_cot[:, None, :].astype(jnp.float32)).astype(jnp.bfloat16)
    grad_out = jnp.dot(
        pick.T, scaled.reshape(-1, features), preferred_element_type=jnp.float32
    ).astype(jnp.bfloat16)
    grads_in = exchange(grad_out.reshape(experts, capacity, features)).reshape(-1, features)

    pre_gate, pre_up, activation = hidden_rows(slot_rows, gate_weight, up_weight)
    result = jnp.dot(activation, down_weight, preferred_element_type=jnp.float32).astype(
        jnp.bfloat16
    )
    pre_gate, pre_up, activation, result = lax.optimization_barrier(
        (pre_gate, pre_up, activation, result)
    )
    returned = exchange(result.reshape(experts, capacity, features)).reshape(-1, features)
    back_rows, d_gate, d_up = backward_rows(
        grads_in, pre_gate, pre_up, gate_weight, up_weight, down_weight
    )
    returned_grad = exchange(back_rows.reshape(experts, capacity, features)).reshape(-1, features)

    picked = jnp.einsum("tkp,pd->tkd", pick3, returned, preferred_element_type=jnp.float32)
    combined = jnp.einsum("tk,tkd->td", gate_probs, picked).astype(jnp.bfloat16)
    grad_tokens = jnp.dot(owner, returned_grad, preferred_element_type=jnp.float32).astype(
        jnp.bfloat16
    )
    gate_up_grad = jnp.concatenate([d_gate, d_up], axis=1)
    gate_up_sum = lax.psum_scatter(
        outer_sum(slot_rows, gate_up_grad).astype(jnp.bfloat16),
        "replica",
        scatter_dimension=0,
        tiled=True,
    ).astype(jnp.float32)
    down_sum = lax.psum_scatter(
        outer_sum(activation, grads_in).astype(jnp.bfloat16),
        "replica",
        scatter_dimension=0,
        tiled=True,
    )
    grad_gate = gate_up_sum[:, :hidden].astype(jnp.bfloat16)[None]
    grad_up = gate_up_sum[:, hidden:].astype(jnp.bfloat16)[None]
    grad_down = down_sum[None]
    return (combined, grad_tokens, grad_gate, grad_up, grad_down)


def solution(mesh):
    placed = (
        P(("expert", "replica"), None),
        P(("expert", "replica"), None),
        P(("expert", "replica"), None),
        P(("expert", "replica"), None),
        P("expert", None, None),
        P("expert", None, None),
        P("expert", None, None),
    )
    return jax.shard_map(
        per_device,
        mesh=mesh,
        in_specs=placed,
        out_specs=(
            P(("expert", "replica"), None),
            P(("expert", "replica"), None),
            P("expert", "replica", None),
            P("expert", "replica", None),
            P("expert", "replica", None),
        ),
        check_vma=False,
    )
```

```python
import jax
import jax.numpy as jnp
from jax import lax
from jax.sharding import PartitionSpec as P


def slots(routes, experts, capacity):
    flat_ids = routes.reshape(-1)
    one_hot = (flat_ids[:, None] == jnp.arange(experts, dtype=jnp.int32)[None, :]).astype(jnp.int32)
    before = jnp.cumsum(one_hot, axis=0) - one_hot
    slot_rank = jnp.sum(before * one_hot, axis=1)
    return flat_ids * capacity + slot_rank


def hidden_rows(token_rows, gate_weight, up_weight):
    pre_gate = jnp.dot(token_rows, gate_weight, preferred_element_type=jnp.float32)
    pre_up = jnp.dot(token_rows, up_weight, preferred_element_type=jnp.float32)
    activation = (jax.nn.silu(pre_gate) * pre_up).astype(jnp.bfloat16)
    return (pre_gate, pre_up, activation)


def backward_rows(grad_rows, pre_gate, pre_up, gate_weight, up_weight, down_weight):
    contract = (((1,), (1,)), ((), ()))
    d_hidden = lax.dot_general(grad_rows, down_weight, contract, preferred_element_type=jnp.float32)
    sigmoid_gate = jax.nn.sigmoid(pre_gate)
    d_gate = (d_hidden * pre_up * sigmoid_gate * (1.0 + pre_gate * (1.0 - sigmoid_gate))).astype(
        jnp.bfloat16
    )
    d_up = (d_hidden * pre_gate * sigmoid_gate).astype(jnp.bfloat16)
    back_rows = lax.dot_general(d_gate, gate_weight, contract, preferred_element_type=jnp.float32)
    back_rows = back_rows + lax.dot_general(
        d_up, up_weight, contract, preferred_element_type=jnp.float32
    )
    return (back_rows.astype(jnp.bfloat16), d_gate, d_up)


def outer_sum(left, right):
    return lax.dot_general(
        left, right, (((0,), (0,)), ((), ())), preferred_element_type=jnp.float32
    )


def exchange(blocks):
    return lax.all_to_all(blocks, "expert", split_axis=0, concat_axis=0, tiled=True)


def ring_reduce_scatter(part, direction):
    n = lax.axis_size("replica")
    me = lax.axis_index("replica")
    table = part.reshape((n, part.shape[0] // n) + part.shape[1:])
    perm = [(i, (i + direction) % n) for i in range(n)]

    def own(step):
        return lax.dynamic_index_in_dim(table, (me - direction * (step + 1)) % n, 0, False)

    acc = own(0)
    for step in range(1, n):
        acc = lax.ppermute(acc, "replica", perm)
        acc = (acc.astype(jnp.float32) + own(step).astype(jnp.float32)).astype(jnp.bfloat16)
    return acc


def per_device(tokens, route_ids, gate_probs, out_cot, w_gate, w_up, w_down):
    experts = lax.axis_size("expert")
    tok_rows, features = tokens.shape
    top_count = route_ids.shape[1]
    hidden = w_gate.shape[2]
    capacity = max(2, tok_rows * top_count * 4 // (3 * experts))
    total_rows = experts * capacity
    positions = slots(route_ids, experts, capacity)
    gate_weight = w_gate[0]
    up_weight = w_up[0]
    down_weight = w_down[0]
    pick = (positions[:, None] == jnp.arange(total_rows, dtype=positions.dtype)[None, :]).astype(
        jnp.bfloat16
    )
    pick3 = pick.reshape(tok_rows, top_count, total_rows)
    owner = jnp.sum(pick3, axis=1)
    outgoing = jnp.dot(owner.T, tokens, preferred_element_type=jnp.float32).astype(jnp.bfloat16)
    slot_rows = exchange(outgoing.reshape(experts, capacity, features)).reshape(-1, features)
    scaled = (gate_probs[:, :, None] * out_cot[:, None, :].astype(jnp.float32)).astype(jnp.bfloat16)
    grad_out = jnp.dot(
        pick.T, scaled.reshape(-1, features), preferred_element_type=jnp.float32
    ).astype(jnp.bfloat16)
    grads_in = exchange(grad_out.reshape(experts, capacity, features)).reshape(-1, features)

    pre_gate, pre_up, activation = hidden_rows(slot_rows, gate_weight, up_weight)
    result = jnp.dot(activation, down_weight, preferred_element_type=jnp.float32).astype(
        jnp.bfloat16
    )
    pre_gate, pre_up, activation, result = lax.optimization_barrier(
        (pre_gate, pre_up, activation, result)
    )
    returned = exchange(result.reshape(experts, capacity, features)).reshape(-1, features)
    back_rows, d_gate, d_up = backward_rows(
        grads_in, pre_gate, pre_up, gate_weight, up_weight, down_weight
    )
    returned_grad = exchange(back_rows.reshape(experts, capacity, features)).reshape(-1, features)

    picked = jnp.einsum("tkp,pd->tkd", pick3, returned, preferred_element_type=jnp.float32)
    combined = jnp.einsum("tk,tkd->td", gate_probs, picked).astype(jnp.bfloat16)
    grad_tokens = jnp.dot(owner, returned_grad, preferred_element_type=jnp.float32).astype(
        jnp.bfloat16
    )
    half = features // 2
    grad_gate = ring_reduce_scatter(outer_sum(slot_rows, d_gate).astype(jnp.bfloat16), 1)[None]
    grad_up = ring_reduce_scatter(outer_sum(slot_rows, d_up).astype(jnp.bfloat16), -1)[None]
    part_down = outer_sum(activation, grads_in).astype(jnp.bfloat16)
    grad_down = jnp.concatenate(
        [
            ring_reduce_scatter(part_down[:, :half], 1),
            ring_reduce_scatter(part_down[:, half:], -1),
        ],
        axis=1,
    )[None]
    return (combined, grad_tokens, grad_gate, grad_up, grad_down)


def solution(mesh):
    placed = (
        P(("expert", "replica"), None),
        P(("expert", "replica"), None),
        P(("expert", "replica"), None),
        P(("expert", "replica"), None),
        P("expert", None, None),
        P("expert", None, None),
        P("expert", None, None),
    )
    return jax.shard_map(
        per_device,
        mesh=mesh,
        in_specs=placed,
        out_specs=(
            P(("expert", "replica"), None),
            P(("expert", "replica"), None),
            P("expert", "replica", None),
            P("expert", "replica", None),
            P("expert", "replica", None),
        ),
        check_vma=False,
    )
```

```python
import jax
import jax.numpy as jnp
from jax import lax
from jax.sharding import PartitionSpec as P


def slots(routes, experts, capacity):
    flat_ids = routes.reshape(-1)
    one_hot = (flat_ids[:, None] == jnp.arange(experts, dtype=jnp.int32)[None, :]).astype(jnp.int32)
    before = jnp.cumsum(one_hot, axis=0) - one_hot
    slot_rank = jnp.sum(before * one_hot, axis=1)
    return flat_ids * capacity + slot_rank


def hidden_rows(token_rows, gate_weight, up_weight):
    pre_gate = jnp.dot(token_rows, gate_weight, preferred_element_type=jnp.float32)
    pre_up = jnp.dot(token_rows, up_weight, preferred_element_type=jnp.float32)
    activation = (jax.nn.silu(pre_gate) * pre_up).astype(jnp.bfloat16)
    return (pre_gate, pre_up, activation)


def backward_rows(grad_rows, pre_gate, pre_up, gate_weight, up_weight, down_weight):
    contract = (((1,), (1,)), ((), ()))
    d_hidden = lax.dot_general(grad_rows, down_weight, contract, preferred_element_type=jnp.float32)
    sigmoid_gate = jax.nn.sigmoid(pre_gate)
    d_gate = (d_hidden * pre_up * sigmoid_gate * (1.0 + pre_gate * (1.0 - sigmoid_gate))).astype(
        jnp.bfloat16
    )
    d_up = (d_hidden * pre_gate * sigmoid_gate).astype(jnp.bfloat16)
    back_rows = lax.dot_general(d_gate, gate_weight, contract, preferred_element_type=jnp.float32)
    back_rows = back_rows + lax.dot_general(
        d_up, up_weight, contract, preferred_element_type=jnp.float32
    )
    return (back_rows.astype(jnp.bfloat16), d_gate, d_up)


def outer_sum(left, right):
    return lax.dot_general(
        left, right, (((0,), (0,)), ((), ())), preferred_element_type=jnp.float32
    )


def exchange(blocks):
    return lax.all_to_all(blocks, "expert", split_axis=0, concat_axis=0, tiled=True)


def ring_reduce_scatter(part, direction):
    n = lax.axis_size("replica")
    me = lax.axis_index("replica")
    table = part.reshape((n, part.shape[0] // n) + part.shape[1:])
    perm = [(i, (i + direction) % n) for i in range(n)]

    def own(step):
        return lax.dynamic_index_in_dim(table, (me - direction * (step + 1)) % n, 0, False)

    acc = own(0)
    for step in range(1, n):
        acc = lax.ppermute(acc, "replica", perm)
        acc = (acc.astype(jnp.float32) + own(step).astype(jnp.float32)).astype(jnp.bfloat16)
    return acc


def per_device(tokens, route_ids, gate_probs, out_cot, w_gate, w_up, w_down):
    experts = lax.axis_size("expert")
    tok_rows, features = tokens.shape
    top_count = route_ids.shape[1]
    hidden = w_gate.shape[2]
    capacity = max(2, tok_rows * top_count * 4 // (3 * experts))
    total_rows = experts * capacity
    positions = slots(route_ids, experts, capacity)
    gate_weight = w_gate[0]
    up_weight = w_up[0]
    down_weight = w_down[0]
    pick = (positions[:, None] == jnp.arange(total_rows, dtype=positions.dtype)[None, :]).astype(
        jnp.bfloat16
    )
    pick3 = pick.reshape(tok_rows, top_count, total_rows)
    owner = jnp.sum(pick3, axis=1)
    outgoing = jnp.dot(owner.T, tokens, preferred_element_type=jnp.float32).astype(jnp.bfloat16)
    slot_rows = exchange(outgoing.reshape(experts, capacity, features)).reshape(-1, features)
    scaled = (gate_probs[:, :, None] * out_cot[:, None, :].astype(jnp.float32)).astype(jnp.bfloat16)
    grad_out = jnp.dot(
        pick.T, scaled.reshape(-1, features), preferred_element_type=jnp.float32
    ).astype(jnp.bfloat16)
    grads_in = exchange(grad_out.reshape(experts, capacity, features)).reshape(-1, features)

    pre_gate, pre_up, activation = hidden_rows(slot_rows, gate_weight, up_weight)
    result = jnp.dot(activation, down_weight, preferred_element_type=jnp.float32).astype(
        jnp.bfloat16
    )
    pre_gate, pre_up, activation, result = lax.optimization_barrier(
        (pre_gate, pre_up, activation, result)
    )
    returned = exchange(result.reshape(experts, capacity, features)).reshape(-1, features)
    back_rows, d_gate, d_up = backward_rows(
        grads_in, pre_gate, pre_up, gate_weight, up_weight, down_weight
    )
    returned_grad = exchange(back_rows.reshape(experts, capacity, features)).reshape(-1, features)

    picked = jnp.einsum("tkp,pd->tkd", pick3, returned, preferred_element_type=jnp.float32)
    combined = jnp.einsum("tk,tkd->td", gate_probs, picked).astype(jnp.bfloat16)
    grad_tokens = jnp.dot(owner, returned_grad, preferred_element_type=jnp.float32).astype(
        jnp.bfloat16
    )
    replicas = lax.axis_size("replica")
    half = features // 2
    part_down = outer_sum(activation, grads_in).astype(jnp.bfloat16)
    down_rows = part_down.shape[0] // replicas
    down_halves = [
        part_down[:, :half].reshape(replicas, down_rows * half // hidden, hidden),
        part_down[:, half:].reshape(replicas, down_rows * half // hidden, hidden),
    ]
    sums = []
    for direction, wide, down_half in zip((1, -1), (d_gate, d_up), down_halves):
        part = outer_sum(slot_rows, wide).astype(jnp.bfloat16)
        table = jnp.concatenate([part.reshape(replicas, -1, hidden), down_half], axis=1)
        sums.append(ring_reduce_scatter(table.reshape(-1, hidden), direction))
    rows = features // replicas
    grad_gate = sums[0][:rows][None]
    grad_up = sums[1][:rows][None]
    grad_down = jnp.concatenate(
        [sums[0][rows:].reshape(down_rows, half), sums[1][rows:].reshape(down_rows, half)], axis=1
    )[None]
    return (combined, grad_tokens, grad_gate, grad_up, grad_down)


def solution(mesh):
    placed = (
        P(("expert", "replica"), None),
        P(("expert", "replica"), None),
        P(("expert", "replica"), None),
        P(("expert", "replica"), None),
        P("expert", None, None),
        P("expert", None, None),
        P("expert", None, None),
    )
    return jax.shard_map(
        per_device,
        mesh=mesh,
        in_specs=placed,
        out_specs=(
            P(("expert", "replica"), None),
            P(("expert", "replica"), None),
            P("expert", "replica", None),
            P("expert", "replica", None),
            P("expert", "replica", None),
        ),
        check_vma=False,
    )
```

```python
import jax
import jax.numpy as jnp
from jax import lax
from jax.sharding import PartitionSpec as P


def slots(routes, experts, capacity):
    flat_ids = routes.reshape(-1)
    one_hot = (flat_ids[:, None] == jnp.arange(experts, dtype=jnp.int32)[None, :]).astype(jnp.int32)
    before = jnp.cumsum(one_hot, axis=0) - one_hot
    slot_rank = jnp.sum(before * one_hot, axis=1)
    return flat_ids * capacity + slot_rank


def hidden_rows(token_rows, gate_weight, up_weight):
    pre_gate = jnp.dot(token_rows, gate_weight, preferred_element_type=jnp.float32)
    pre_up = jnp.dot(token_rows, up_weight, preferred_element_type=jnp.float32)
    activation = (jax.nn.silu(pre_gate) * pre_up).astype(jnp.bfloat16)
    return (pre_gate, pre_up, activation)


def backward_rows(grad_rows, pre_gate, pre_up, gate_weight, up_weight, down_weight):
    contract = (((1,), (1,)), ((), ()))
    d_hidden = lax.dot_general(grad_rows, down_weight, contract, preferred_element_type=jnp.float32)
    sigmoid_gate = jax.nn.sigmoid(pre_gate)
    d_gate = (d_hidden * pre_up * sigmoid_gate * (1.0 + pre_gate * (1.0 - sigmoid_gate))).astype(
        jnp.bfloat16
    )
    d_up = (d_hidden * pre_gate * sigmoid_gate).astype(jnp.bfloat16)
    back_rows = lax.dot_general(d_gate, gate_weight, contract, preferred_element_type=jnp.float32)
    back_rows = back_rows + lax.dot_general(
        d_up, up_weight, contract, preferred_element_type=jnp.float32
    )
    return (back_rows.astype(jnp.bfloat16), d_gate, d_up)


def outer_sum(left, right):
    return lax.dot_general(
        left, right, (((0,), (0,)), ((), ())), preferred_element_type=jnp.float32
    )


def exchange(blocks):
    return lax.all_to_all(blocks, "expert", split_axis=0, concat_axis=0, tiled=True)


def ring_reduce_scatter(part, direction):
    n = lax.axis_size("replica")
    me = lax.axis_index("replica")
    table = part.reshape((n, part.shape[0] // n) + part.shape[1:])
    perm = [(i, (i + direction) % n) for i in range(n)]

    def own(step):
        return lax.dynamic_index_in_dim(table, (me - direction * (step + 1)) % n, 0, False)

    acc = own(0)
    for step in range(1, n):
        acc = lax.ppermute(acc, "replica", perm)
        acc = (acc.astype(jnp.float32) + own(step).astype(jnp.float32)).astype(jnp.bfloat16)
    return acc


def per_device(tokens, route_ids, gate_probs, out_cot, w_gate, w_up, w_down):
    experts = lax.axis_size("expert")
    tok_rows, features = tokens.shape
    top_count = route_ids.shape[1]
    hidden = w_gate.shape[2]
    capacity = max(2, tok_rows * top_count * 4 // (3 * experts))
    total_rows = experts * capacity
    positions = slots(route_ids, experts, capacity)
    gate_weight = w_gate[0]
    up_weight = w_up[0]
    down_weight = w_down[0]
    pick = (positions[:, None] == jnp.arange(total_rows, dtype=positions.dtype)[None, :]).astype(
        jnp.bfloat16
    )
    pick3 = pick.reshape(tok_rows, top_count, total_rows)
    owner = jnp.sum(pick3, axis=1)
    outgoing = jnp.dot(owner.T, tokens, preferred_element_type=jnp.float32).astype(jnp.bfloat16)
    slot_rows = exchange(outgoing.reshape(experts, capacity, features)).reshape(-1, features)
    scaled = (gate_probs[:, :, None] * out_cot[:, None, :].astype(jnp.float32)).astype(jnp.bfloat16)
    grad_out = jnp.dot(
        pick.T, scaled.reshape(-1, features), preferred_element_type=jnp.float32
    ).astype(jnp.bfloat16)
    grads_in = exchange(grad_out.reshape(experts, capacity, features)).reshape(-1, features)

    pre_gate, pre_up, activation = hidden_rows(slot_rows, gate_weight, up_weight)
    result = jnp.dot(activation, down_weight, preferred_element_type=jnp.float32).astype(
        jnp.bfloat16
    )
    pre_gate, pre_up, activation, result = lax.optimization_barrier(
        (pre_gate, pre_up, activation, result)
    )
    returned = exchange(result.reshape(experts, capacity, features)).reshape(-1, features)
    back_rows, d_gate, d_up = backward_rows(
        grads_in, pre_gate, pre_up, gate_weight, up_weight, down_weight
    )

    replicas = lax.axis_size("replica")
    half = features // 2
    part_down = outer_sum(activation, grads_in).astype(jnp.bfloat16)
    down_rows = part_down.shape[0] // replicas
    down_halves = [
        part_down[:, :half].reshape(replicas, down_rows * half // hidden, hidden),
        part_down[:, half:].reshape(replicas, down_rows * half // hidden, hidden),
    ]
    tables = []
    for wide, down_half in zip((d_gate, d_up), down_halves):
        part = outer_sum(slot_rows, wide).astype(jnp.bfloat16)
        table = jnp.concatenate([part.reshape(replicas, -1, hidden), down_half], axis=1)
        tables.append(table.reshape(-1, hidden))
    tables, back_rows = lax.optimization_barrier((tables, back_rows))
    returned_grad = exchange(back_rows.reshape(experts, capacity, features)).reshape(-1, features)
    sums = [ring_reduce_scatter(table, direction) for direction, table in zip((1, -1), tables)]
    rows = features // replicas
    grad_gate = sums[0][:rows][None]
    grad_up = sums[1][:rows][None]
    grad_down = jnp.concatenate(
        [sums[0][rows:].reshape(down_rows, half), sums[1][rows:].reshape(down_rows, half)], axis=1
    )[None]
    picked = jnp.einsum("tkp,pd->tkd", pick3, returned, preferred_element_type=jnp.float32)
    combined = jnp.einsum("tk,tkd->td", gate_probs, picked).astype(jnp.bfloat16)
    grad_tokens = jnp.dot(owner, returned_grad, preferred_element_type=jnp.float32).astype(
        jnp.bfloat16
    )
    return (combined, grad_tokens, grad_gate, grad_up, grad_down)


def solution(mesh):
    placed = (
        P(("expert", "replica"), None),
        P(("expert", "replica"), None),
        P(("expert", "replica"), None),
        P(("expert", "replica"), None),
        P("expert", None, None),
        P("expert", None, None),
        P("expert", None, None),
    )
    return jax.shard_map(
        per_device,
        mesh=mesh,
        in_specs=placed,
        out_specs=(
            P(("expert", "replica"), None),
            P(("expert", "replica"), None),
            P("expert", "replica", None),
            P("expert", "replica", None),
            P("expert", "replica", None),
        ),
        check_vma=False,
    )
```

```python
import jax
import jax.numpy as jnp
from jax import lax
from jax.sharding import PartitionSpec as P


def slots(routes, experts, capacity):
    flat_ids = routes.reshape(-1)
    one_hot = (flat_ids[:, None] == jnp.arange(experts, dtype=jnp.int32)[None, :]).astype(jnp.int32)
    before = jnp.cumsum(one_hot, axis=0) - one_hot
    slot_rank = jnp.sum(before * one_hot, axis=1)
    return flat_ids * capacity + slot_rank


def hidden_rows(token_rows, gate_weight, up_weight):
    pre_gate = jnp.dot(token_rows, gate_weight, preferred_element_type=jnp.float32)
    pre_up = jnp.dot(token_rows, up_weight, preferred_element_type=jnp.float32)
    activation = (jax.nn.silu(pre_gate) * pre_up).astype(jnp.bfloat16)
    return (pre_gate, pre_up, activation)


def backward_rows(grad_rows, pre_gate, pre_up, gate_weight, up_weight, down_weight):
    contract = (((1,), (1,)), ((), ()))
    d_hidden = lax.dot_general(grad_rows, down_weight, contract, preferred_element_type=jnp.float32)
    sigmoid_gate = jax.nn.sigmoid(pre_gate)
    d_gate = (d_hidden * pre_up * sigmoid_gate * (1.0 + pre_gate * (1.0 - sigmoid_gate))).astype(
        jnp.bfloat16
    )
    d_up = (d_hidden * pre_gate * sigmoid_gate).astype(jnp.bfloat16)
    back_rows = lax.dot_general(d_gate, gate_weight, contract, preferred_element_type=jnp.float32)
    back_rows = back_rows + lax.dot_general(
        d_up, up_weight, contract, preferred_element_type=jnp.float32
    )
    return (back_rows.astype(jnp.bfloat16), d_gate, d_up)


def outer_sum(left, right):
    return lax.dot_general(
        left, right, (((0,), (0,)), ((), ())), preferred_element_type=jnp.float32
    )


def exchange(blocks):
    return lax.all_to_all(blocks, "expert", split_axis=0, concat_axis=0, tiled=True)


def per_device(tokens, route_ids, gate_probs, out_cot, w_gate, w_up, w_down):
    experts = lax.axis_size("expert")
    tok_rows, features = tokens.shape
    top_count = route_ids.shape[1]
    hidden = w_gate.shape[2]
    capacity = max(2, tok_rows * top_count * 4 // (3 * experts))
    total_rows = experts * capacity
    positions = slots(route_ids, experts, capacity)
    gate_weight = w_gate[0]
    up_weight = w_up[0]
    down_weight = w_down[0]
    pick = (positions[:, None] == jnp.arange(total_rows, dtype=positions.dtype)[None, :]).astype(
        jnp.bfloat16
    )
    pick3 = pick.reshape(tok_rows, top_count, total_rows)
    owner = jnp.sum(pick3, axis=1)
    outgoing = jnp.dot(owner.T, tokens, preferred_element_type=jnp.float32).astype(jnp.bfloat16)
    slot_rows = exchange(outgoing.reshape(experts, capacity, features)).reshape(-1, features)
    scaled = (gate_probs[:, :, None] * out_cot[:, None, :].astype(jnp.float32)).astype(jnp.bfloat16)
    grad_out = jnp.dot(
        pick.T, scaled.reshape(-1, features), preferred_element_type=jnp.float32
    ).astype(jnp.bfloat16)
    grads_in = exchange(grad_out.reshape(experts, capacity, features)).reshape(-1, features)

    pre_gate, pre_up, activation = hidden_rows(slot_rows, gate_weight, up_weight)
    result = jnp.dot(activation, down_weight, preferred_element_type=jnp.float32).astype(
        jnp.bfloat16
    )
    pre_gate, pre_up, activation, result = lax.optimization_barrier(
        (pre_gate, pre_up, activation, result)
    )
    returned = exchange(result.reshape(experts, capacity, features)).reshape(-1, features)
    back_rows, d_gate, d_up = backward_rows(
        grads_in, pre_gate, pre_up, gate_weight, up_weight, down_weight
    )
    returned_grad = exchange(back_rows.reshape(experts, capacity, features)).reshape(-1, features)

    picked = jnp.einsum("tkp,pd->tkd", pick3, returned, preferred_element_type=jnp.float32)
    combined = jnp.einsum("tk,tkd->td", gate_probs, picked).astype(jnp.bfloat16)
    grad_tokens = jnp.dot(owner, returned_grad, preferred_element_type=jnp.float32).astype(
        jnp.bfloat16
    )
    grad_gate = lax.psum_scatter(
        outer_sum(slot_rows, d_gate).astype(jnp.bfloat16), "replica", scatter_dimension=0, tiled=True
    )[None]
    grad_up = lax.psum_scatter(
        outer_sum(slot_rows, d_up).astype(jnp.bfloat16), "replica", scatter_dimension=0, tiled=True
    )[None]
    down_sum = lax.psum_scatter(
        outer_sum(activation, grads_in).astype(jnp.bfloat16),
        "replica",
        scatter_dimension=0,
        tiled=True,
    )
    grad_down = down_sum[None]
    return (combined, grad_tokens, grad_gate, grad_up, grad_down)


def solution(mesh):
    placed = (
        P(("expert", "replica"), None),
        P(("expert", "replica"), None),
        P(("expert", "replica"), None),
        P(("expert", "replica"), None),
        P("expert", None, None),
        P("expert", None, None),
        P("expert", None, None),
    )
    return jax.shard_map(
        per_device,
        mesh=mesh,
        in_specs=placed,
        out_specs=(
            P(("expert", "replica"), None),
            P(("expert", "replica"), None),
            P("expert", "replica", None),
            P("expert", "replica", None),
            P("expert", "replica", None),
        ),
        check_vma=False,
    )
```

```python
import jax
import jax.numpy as jnp
from jax import lax
from jax.sharding import PartitionSpec as P


def slots(routes, experts, capacity):
    flat_ids = routes.reshape(-1)
    one_hot = (flat_ids[:, None] == jnp.arange(experts, dtype=jnp.int32)[None, :]).astype(jnp.int32)
    before = jnp.cumsum(one_hot, axis=0) - one_hot
    slot_rank = jnp.sum(before * one_hot, axis=1)
    return flat_ids * capacity + slot_rank


def hidden_rows(token_rows, gate_weight, up_weight):
    pre_gate = jnp.dot(token_rows, gate_weight, preferred_element_type=jnp.float32)
    pre_up = jnp.dot(token_rows, up_weight, preferred_element_type=jnp.float32)
    activation = (jax.nn.silu(pre_gate) * pre_up).astype(jnp.bfloat16)
    return (pre_gate, pre_up, activation)


def backward_rows(grad_rows, pre_gate, pre_up, gate_weight, up_weight, down_weight):
    contract = (((1,), (1,)), ((), ()))
    d_hidden = lax.dot_general(grad_rows, down_weight, contract, preferred_element_type=jnp.float32)
    sigmoid_gate = jax.nn.sigmoid(pre_gate)
    d_gate = (d_hidden * pre_up * sigmoid_gate * (1.0 + pre_gate * (1.0 - sigmoid_gate))).astype(
        jnp.bfloat16
    )
    d_up = (d_hidden * pre_gate * sigmoid_gate).astype(jnp.bfloat16)
    back_rows = lax.dot_general(d_gate, gate_weight, contract, preferred_element_type=jnp.float32)
    back_rows = back_rows + lax.dot_general(
        d_up, up_weight, contract, preferred_element_type=jnp.float32
    )
    return (back_rows.astype(jnp.bfloat16), d_gate, d_up)


def outer_sum(left, right):
    return lax.dot_general(
        left, right, (((0,), (0,)), ((), ())), preferred_element_type=jnp.float32
    )


def exchange(blocks):
    return lax.all_to_all(blocks, "expert", split_axis=0, concat_axis=0, tiled=True)


def ring_reduce_scatter(part, direction):
    n = lax.axis_size("replica")
    me = lax.axis_index("replica")
    table = part.reshape((n, part.shape[0] // n) + part.shape[1:])
    perm = [(i, (i + direction) % n) for i in range(n)]

    def own(step):
        return lax.dynamic_index_in_dim(table, (me - direction * (step + 1)) % n, 0, False)

    acc = own(0)
    for step in range(1, n):
        acc = lax.ppermute(acc, "replica", perm)
        acc = (acc.astype(jnp.float32) + own(step).astype(jnp.float32)).astype(jnp.bfloat16)
    return acc


def per_device(tokens, route_ids, gate_probs, out_cot, w_gate, w_up, w_down):
    experts = lax.axis_size("expert")
    tok_rows, features = tokens.shape
    top_count = route_ids.shape[1]
    hidden = w_gate.shape[2]
    capacity = max(2, tok_rows * top_count * 4 // (3 * experts))
    total_rows = experts * capacity
    positions = slots(route_ids, experts, capacity)
    gate_weight = w_gate[0]
    up_weight = w_up[0]
    down_weight = w_down[0]
    pick = (positions[:, None] == jnp.arange(total_rows, dtype=positions.dtype)[None, :]).astype(
        jnp.bfloat16
    )
    pick3 = pick.reshape(tok_rows, top_count, total_rows)
    owner = jnp.sum(pick3, axis=1)
    outgoing = jnp.dot(owner.T, tokens, preferred_element_type=jnp.float32).astype(jnp.bfloat16)
    slot_rows = exchange(outgoing.reshape(experts, capacity, features)).reshape(-1, features)
    scaled = (gate_probs[:, :, None] * out_cot[:, None, :].astype(jnp.float32)).astype(jnp.bfloat16)
    grad_out = jnp.dot(
        pick.T, scaled.reshape(-1, features), preferred_element_type=jnp.float32
    ).astype(jnp.bfloat16)
    grads_in = exchange(grad_out.reshape(experts, capacity, features)).reshape(-1, features)

    pre_gate, pre_up, activation = hidden_rows(slot_rows, gate_weight, up_weight)
    result = jnp.dot(activation, down_weight, preferred_element_type=jnp.float32).astype(
        jnp.bfloat16
    )
    pre_gate, pre_up, activation, result = lax.optimization_barrier(
        (pre_gate, pre_up, activation, result)
    )
    returned = exchange(result.reshape(experts, capacity, features)).reshape(-1, features)
    back_rows, d_gate, d_up = backward_rows(
        grads_in, pre_gate, pre_up, gate_weight, up_weight, down_weight
    )
    returned_grad = exchange(back_rows.reshape(experts, capacity, features)).reshape(-1, features)

    grad_gate = lax.psum_scatter(
        outer_sum(slot_rows, d_gate).astype(jnp.bfloat16), "replica", scatter_dimension=0, tiled=True
    )[None]
    grad_up = lax.psum_scatter(
        outer_sum(slot_rows, d_up).astype(jnp.bfloat16), "replica", scatter_dimension=0, tiled=True
    )[None]
    part_down, returned = lax.optimization_barrier(
        (outer_sum(activation, grads_in).astype(jnp.bfloat16), returned)
    )
    half = features // 2
    grad_down = jnp.concatenate(
        [
            ring_reduce_scatter(part_down[:, :half], 1),
            ring_reduce_scatter(part_down[:, half:], -1),
        ],
        axis=1,
    )[None]
    picked = jnp.einsum("tkp,pd->tkd", pick3, returned, preferred_element_type=jnp.float32)
    combined = jnp.einsum("tk,tkd->td", gate_probs, picked).astype(jnp.bfloat16)
    grad_tokens = jnp.dot(owner, returned_grad, preferred_element_type=jnp.float32).astype(
        jnp.bfloat16
    )
    return (combined, grad_tokens, grad_gate, grad_up, grad_down)


def solution(mesh):
    placed = (
        P(("expert", "replica"), None),
        P(("expert", "replica"), None),
        P(("expert", "replica"), None),
        P(("expert", "replica"), None),
        P("expert", None, None),
        P("expert", None, None),
        P("expert", None, None),
    )
    return jax.shard_map(
        per_device,
        mesh=mesh,
        in_specs=placed,
        out_specs=(
            P(("expert", "replica"), None),
            P(("expert", "replica"), None),
            P("expert", "replica", None),
            P("expert", "replica", None),
            P("expert", "replica", None),
        ),
        check_vma=False,
    )
```

```python
import jax
import jax.numpy as jnp
from jax import lax
from jax.sharding import PartitionSpec as P


def slots(routes, experts, capacity):
    flat_ids = routes.reshape(-1)
    one_hot = (flat_ids[:, None] == jnp.arange(experts, dtype=jnp.int32)[None, :]).astype(jnp.int32)
    before = jnp.cumsum(one_hot, axis=0) - one_hot
    slot_rank = jnp.sum(before * one_hot, axis=1)
    return flat_ids * capacity + slot_rank


def hidden_rows(token_rows, gate_weight, up_weight):
    pre_gate = jnp.dot(token_rows, gate_weight, preferred_element_type=jnp.float32)
    pre_up = jnp.dot(token_rows, up_weight, preferred_element_type=jnp.float32)
    activation = (jax.nn.silu(pre_gate) * pre_up).astype(jnp.bfloat16)
    return (pre_gate, pre_up, activation)


def backward_rows(grad_rows, pre_gate, pre_up, gate_weight, up_weight, down_weight):
    contract = (((1,), (1,)), ((), ()))
    d_hidden = lax.dot_general(grad_rows, down_weight, contract, preferred_element_type=jnp.float32)
    sigmoid_gate = jax.nn.sigmoid(pre_gate)
    d_gate = (d_hidden * pre_up * sigmoid_gate * (1.0 + pre_gate * (1.0 - sigmoid_gate))).astype(
        jnp.bfloat16
    )
    d_up = (d_hidden * pre_gate * sigmoid_gate).astype(jnp.bfloat16)
    back_rows = lax.dot_general(d_gate, gate_weight, contract, preferred_element_type=jnp.float32)
    back_rows = back_rows + lax.dot_general(
        d_up, up_weight, contract, preferred_element_type=jnp.float32
    )
    return (back_rows.astype(jnp.bfloat16), d_gate, d_up)


def outer_sum(left, right):
    return lax.dot_general(
        left, right, (((0,), (0,)), ((), ())), preferred_element_type=jnp.float32
    )


def exchange(blocks):
    return lax.all_to_all(blocks, "expert", split_axis=0, concat_axis=0, tiled=True)


def ring_reduce_scatter(part, direction):
    n = lax.axis_size("replica")
    me = lax.axis_index("replica")
    table = part.reshape((n, part.shape[0] // n) + part.shape[1:])
    perm = [(i, (i + direction) % n) for i in range(n)]

    def own(step):
        return lax.dynamic_index_in_dim(table, (me - direction * (step + 1)) % n, 0, False)

    acc = own(0)
    for step in range(1, n):
        acc = lax.ppermute(acc, "replica", perm)
        acc = (acc.astype(jnp.float32) + own(step).astype(jnp.float32)).astype(jnp.bfloat16)
    return acc


def per_device(tokens, route_ids, gate_probs, out_cot, w_gate, w_up, w_down):
    experts = lax.axis_size("expert")
    tok_rows, features = tokens.shape
    top_count = route_ids.shape[1]
    hidden = w_gate.shape[2]
    capacity = max(2, tok_rows * top_count * 4 // (3 * experts))
    total_rows = experts * capacity
    positions = slots(route_ids, experts, capacity)
    gate_weight = w_gate[0]
    up_weight = w_up[0]
    down_weight = w_down[0]
    pick = (positions[:, None] == jnp.arange(total_rows, dtype=positions.dtype)[None, :]).astype(
        jnp.bfloat16
    )
    pick3 = pick.reshape(tok_rows, top_count, total_rows)
    owner = jnp.sum(pick3, axis=1)
    outgoing = jnp.dot(owner.T, tokens, preferred_element_type=jnp.float32).astype(jnp.bfloat16)
    slot_rows = exchange(outgoing.reshape(experts, capacity, features)).reshape(-1, features)
    scaled = (gate_probs[:, :, None] * out_cot[:, None, :].astype(jnp.float32)).astype(jnp.bfloat16)
    grad_out = jnp.dot(
        pick.T, scaled.reshape(-1, features), preferred_element_type=jnp.float32
    ).astype(jnp.bfloat16)
    grads_in = exchange(grad_out.reshape(experts, capacity, features)).reshape(-1, features)

    pre_gate, pre_up, activation = hidden_rows(slot_rows, gate_weight, up_weight)
    result = jnp.dot(activation, down_weight, preferred_element_type=jnp.float32).astype(
        jnp.bfloat16
    )
    pre_gate, pre_up, activation, result = lax.optimization_barrier(
        (pre_gate, pre_up, activation, result)
    )
    returned = exchange(result.reshape(experts, capacity, features)).reshape(-1, features)
    back_rows, d_gate, d_up = backward_rows(
        grads_in, pre_gate, pre_up, gate_weight, up_weight, down_weight
    )
    returned_grad = exchange(back_rows.reshape(experts, capacity, features)).reshape(-1, features)

    grad_gate = lax.psum_scatter(
        outer_sum(slot_rows, d_gate).astype(jnp.bfloat16), "replica", scatter_dimension=0, tiled=True
    )[None]
    grad_up = lax.psum_scatter(
        outer_sum(slot_rows, d_up).astype(jnp.bfloat16), "replica", scatter_dimension=0, tiled=True
    )[None]
    part_down, returned = lax.optimization_barrier(
        (outer_sum(activation, grads_in).astype(jnp.bfloat16), returned)
    )
    grad_down = ring_reduce_scatter(part_down, 1)[None]
    picked = jnp.einsum("tkp,pd->tkd", pick3, returned, preferred_element_type=jnp.float32)
    combined = jnp.einsum("tk,tkd->td", gate_probs, picked).astype(jnp.bfloat16)
    grad_tokens = jnp.dot(owner, returned_grad, preferred_element_type=jnp.float32).astype(
        jnp.bfloat16
    )
    return (combined, grad_tokens, grad_gate, grad_up, grad_down)


def solution(mesh):
    placed = (
        P(("expert", "replica"), None),
        P(("expert", "replica"), None),
        P(("expert", "replica"), None),
        P(("expert", "replica"), None),
        P("expert", None, None),
        P("expert", None, None),
        P("expert", None, None),
    )
    return jax.shard_map(
        per_device,
        mesh=mesh,
        in_specs=placed,
        out_specs=(
            P(("expert", "replica"), None),
            P(("expert", "replica"), None),
            P("expert", "replica", None),
            P("expert", "replica", None),
            P("expert", "replica", None),
        ),
        check_vma=False,
    )
```

```python
import jax
import jax.numpy as jnp
from jax import lax
from jax.sharding import PartitionSpec as P


def slots(routes, experts, capacity):
    flat_ids = routes.reshape(-1)
    one_hot = (flat_ids[:, None] == jnp.arange(experts, dtype=jnp.int32)[None, :]).astype(jnp.int32)
    before = jnp.cumsum(one_hot, axis=0) - one_hot
    slot_rank = jnp.sum(before * one_hot, axis=1)
    return flat_ids * capacity + slot_rank


def hidden_rows(token_rows, gate_weight, up_weight):
    pre_gate = jnp.dot(token_rows, gate_weight, preferred_element_type=jnp.float32)
    pre_up = jnp.dot(token_rows, up_weight, preferred_element_type=jnp.float32)
    activation = (jax.nn.silu(pre_gate) * pre_up).astype(jnp.bfloat16)
    return (pre_gate, pre_up, activation)


def backward_rows(grad_rows, pre_gate, pre_up, gate_weight, up_weight, down_weight):
    contract = (((1,), (1,)), ((), ()))
    d_hidden = lax.dot_general(grad_rows, down_weight, contract, preferred_element_type=jnp.float32)
    sigmoid_gate = jax.nn.sigmoid(pre_gate)
    d_gate = (d_hidden * pre_up * sigmoid_gate * (1.0 + pre_gate * (1.0 - sigmoid_gate))).astype(
        jnp.bfloat16
    )
    d_up = (d_hidden * pre_gate * sigmoid_gate).astype(jnp.bfloat16)
    back_rows = lax.dot_general(d_gate, gate_weight, contract, preferred_element_type=jnp.float32)
    back_rows = back_rows + lax.dot_general(
        d_up, up_weight, contract, preferred_element_type=jnp.float32
    )
    return (back_rows.astype(jnp.bfloat16), d_gate, d_up)


def outer_sum(left, right):
    return lax.dot_general(
        left, right, (((0,), (0,)), ((), ())), preferred_element_type=jnp.float32
    )


def exchange(blocks):
    return lax.all_to_all(blocks, "expert", split_axis=0, concat_axis=0, tiled=True)


def chain_reduce_scatter(part):
    n = lax.axis_size("replica")
    me = lax.axis_index("replica")
    table = part.reshape((n, part.shape[0] // n) + part.shape[1:])

    def own(offset):
        return lax.dynamic_index_in_dim(table, (me + offset) % n, 0, False).astype(jnp.float32)

    total = own(0)
    for direction, length in ((1, (n - 1 + 1) // 2), (-1, (n - 1) // 2)):
        if length == 0:
            continue
        perm = [(i, (i + direction) % n) for i in range(n)]
        acc = own(direction * length)
        for step in range(1, length):
            acc = lax.ppermute(acc.astype(jnp.bfloat16), "replica", perm).astype(jnp.float32)
            acc = acc + own(direction * (length - step))
        total = total + lax.ppermute(acc.astype(jnp.bfloat16), "replica", perm).astype(jnp.float32)
    return total.astype(jnp.bfloat16)


def per_device(tokens, route_ids, gate_probs, out_cot, w_gate, w_up, w_down):
    experts = lax.axis_size("expert")
    tok_rows, features = tokens.shape
    top_count = route_ids.shape[1]
    hidden = w_gate.shape[2]
    capacity = max(2, tok_rows * top_count * 4 // (3 * experts))
    total_rows = experts * capacity
    positions = slots(route_ids, experts, capacity)
    gate_weight = w_gate[0]
    up_weight = w_up[0]
    down_weight = w_down[0]
    pick = (positions[:, None] == jnp.arange(total_rows, dtype=positions.dtype)[None, :]).astype(
        jnp.bfloat16
    )
    pick3 = pick.reshape(tok_rows, top_count, total_rows)
    owner = jnp.sum(pick3, axis=1)
    outgoing = jnp.dot(owner.T, tokens, preferred_element_type=jnp.float32).astype(jnp.bfloat16)
    slot_rows = exchange(outgoing.reshape(experts, capacity, features)).reshape(-1, features)
    scaled = (gate_probs[:, :, None] * out_cot[:, None, :].astype(jnp.float32)).astype(jnp.bfloat16)
    grad_out = jnp.dot(
        pick.T, scaled.reshape(-1, features), preferred_element_type=jnp.float32
    ).astype(jnp.bfloat16)
    grads_in = exchange(grad_out.reshape(experts, capacity, features)).reshape(-1, features)

    pre_gate, pre_up, activation = hidden_rows(slot_rows, gate_weight, up_weight)
    result = jnp.dot(activation, down_weight, preferred_element_type=jnp.float32).astype(
        jnp.bfloat16
    )
    pre_gate, pre_up, activation, result = lax.optimization_barrier(
        (pre_gate, pre_up, activation, result)
    )
    returned = exchange(result.reshape(experts, capacity, features)).reshape(-1, features)
    back_rows, d_gate, d_up = backward_rows(
        grads_in, pre_gate, pre_up, gate_weight, up_weight, down_weight
    )
    returned_grad = exchange(back_rows.reshape(experts, capacity, features)).reshape(-1, features)

    grad_gate = lax.psum_scatter(
        outer_sum(slot_rows, d_gate).astype(jnp.bfloat16), "replica", scatter_dimension=0, tiled=True
    )[None]
    grad_up = lax.psum_scatter(
        outer_sum(slot_rows, d_up).astype(jnp.bfloat16), "replica", scatter_dimension=0, tiled=True
    )[None]
    part_down, returned = lax.optimization_barrier(
        (outer_sum(activation, grads_in).astype(jnp.bfloat16), returned)
    )
    grad_down = chain_reduce_scatter(part_down)[None]
    picked = jnp.einsum("tkp,pd->tkd", pick3, returned, preferred_element_type=jnp.float32)
    combined = jnp.einsum("tk,tkd->td", gate_probs, picked).astype(jnp.bfloat16)
    grad_tokens = jnp.dot(owner, returned_grad, preferred_element_type=jnp.float32).astype(
        jnp.bfloat16
    )
    return (combined, grad_tokens, grad_gate, grad_up, grad_down)


def solution(mesh):
    placed = (
        P(("expert", "replica"), None),
        P(("expert", "replica"), None),
        P(("expert", "replica"), None),
        P(("expert", "replica"), None),
        P("expert", None, None),
        P("expert", None, None),
        P("expert", None, None),
    )
    return jax.shard_map(
        per_device,
        mesh=mesh,
        in_specs=placed,
        out_specs=(
            P(("expert", "replica"), None),
            P(("expert", "replica"), None),
            P("expert", "replica", None),
            P("expert", "replica", None),
            P("expert", "replica", None),
        ),
        check_vma=False,
    )
```

```python
import jax
import jax.numpy as jnp
from jax import lax
from jax.sharding import PartitionSpec as P


def slots(routes, experts, capacity):
    flat_ids = routes.reshape(-1)
    one_hot = (flat_ids[:, None] == jnp.arange(experts, dtype=jnp.int32)[None, :]).astype(jnp.int32)
    before = jnp.cumsum(one_hot, axis=0) - one_hot
    slot_rank = jnp.sum(before * one_hot, axis=1)
    return flat_ids * capacity + slot_rank


def hidden_rows(token_rows, gate_weight, up_weight):
    pre_gate = jnp.dot(token_rows, gate_weight, preferred_element_type=jnp.float32)
    pre_up = jnp.dot(token_rows, up_weight, preferred_element_type=jnp.float32)
    activation = (jax.nn.silu(pre_gate) * pre_up).astype(jnp.bfloat16)
    return (pre_gate, pre_up, activation)


def backward_rows(grad_rows, pre_gate, pre_up, gate_weight, up_weight, down_weight):
    contract = (((1,), (1,)), ((), ()))
    d_hidden = lax.dot_general(grad_rows, down_weight, contract, preferred_element_type=jnp.float32)
    sigmoid_gate = jax.nn.sigmoid(pre_gate)
    d_gate = (d_hidden * pre_up * sigmoid_gate * (1.0 + pre_gate * (1.0 - sigmoid_gate))).astype(
        jnp.bfloat16
    )
    d_up = (d_hidden * pre_gate * sigmoid_gate).astype(jnp.bfloat16)
    back_rows = lax.dot_general(d_gate, gate_weight, contract, preferred_element_type=jnp.float32)
    back_rows = back_rows + lax.dot_general(
        d_up, up_weight, contract, preferred_element_type=jnp.float32
    )
    return (back_rows.astype(jnp.bfloat16), d_gate, d_up)


def outer_sum(left, right):
    return lax.dot_general(
        left, right, (((0,), (0,)), ((), ())), preferred_element_type=jnp.float32
    )


def exchange(blocks):
    return lax.all_to_all(blocks, "expert", split_axis=0, concat_axis=0, tiled=True)


def chain_reduce_scatter(part):
    n = lax.axis_size("replica")
    me = lax.axis_index("replica")
    table = part.reshape((n, part.shape[0] // n) + part.shape[1:])

    def own(offset):
        return lax.dynamic_index_in_dim(table, (me + offset) % n, 0, False).astype(jnp.float32)

    total = own(0)
    for direction, length in ((1, (n - 1 + 1) // 2), (-1, (n - 1) // 2)):
        if length == 0:
            continue
        perm = [(i, (i + direction) % n) for i in range(n)]
        acc = own(direction * length)
        for step in range(1, length):
            acc = lax.ppermute(acc.astype(jnp.bfloat16), "replica", perm).astype(jnp.float32)
            acc = acc + own(direction * (length - step))
        total = total + lax.ppermute(acc.astype(jnp.bfloat16), "replica", perm).astype(jnp.float32)
    return total.astype(jnp.bfloat16)


def per_device(tokens, route_ids, gate_probs, out_cot, w_gate, w_up, w_down):
    experts = lax.axis_size("expert")
    tok_rows, features = tokens.shape
    top_count = route_ids.shape[1]
    hidden = w_gate.shape[2]
    capacity = max(2, tok_rows * top_count * 4 // (3 * experts))
    total_rows = experts * capacity
    positions = slots(route_ids, experts, capacity)
    gate_weight = w_gate[0]
    up_weight = w_up[0]
    down_weight = w_down[0]
    pick = (positions[:, None] == jnp.arange(total_rows, dtype=positions.dtype)[None, :]).astype(
        jnp.bfloat16
    )
    pick3 = pick.reshape(tok_rows, top_count, total_rows)
    owner = jnp.sum(pick3, axis=1)
    outgoing = jnp.dot(owner.T, tokens, preferred_element_type=jnp.float32).astype(jnp.bfloat16)
    slot_rows = exchange(outgoing.reshape(experts, capacity, features)).reshape(-1, features)
    scaled = (gate_probs[:, :, None] * out_cot[:, None, :].astype(jnp.float32)).astype(jnp.bfloat16)
    grad_out = jnp.dot(
        pick.T, scaled.reshape(-1, features), preferred_element_type=jnp.float32
    ).astype(jnp.bfloat16)
    grads_in = exchange(grad_out.reshape(experts, capacity, features)).reshape(-1, features)

    pre_gate, pre_up, activation = hidden_rows(slot_rows, gate_weight, up_weight)
    result = jnp.dot(activation, down_weight, preferred_element_type=jnp.float32).astype(
        jnp.bfloat16
    )
    pre_gate, pre_up, activation, result = lax.optimization_barrier(
        (pre_gate, pre_up, activation, result)
    )
    returned = exchange(result.reshape(experts, capacity, features)).reshape(-1, features)
    back_rows, d_gate, d_up = backward_rows(
        grads_in, pre_gate, pre_up, gate_weight, up_weight, down_weight
    )

    grad_gate = lax.psum_scatter(
        outer_sum(slot_rows, d_gate).astype(jnp.bfloat16), "replica", scatter_dimension=0, tiled=True
    )[None]
    grad_up = lax.psum_scatter(
        outer_sum(slot_rows, d_up).astype(jnp.bfloat16), "replica", scatter_dimension=0, tiled=True
    )[None]
    part_down, back_rows = lax.optimization_barrier(
        (outer_sum(activation, grads_in).astype(jnp.bfloat16), back_rows)
    )
    returned_grad = exchange(back_rows.reshape(experts, capacity, features)).reshape(-1, features)
    grad_down = chain_reduce_scatter(part_down)[None]
    picked = jnp.einsum("tkp,pd->tkd", pick3, returned, preferred_element_type=jnp.float32)
    combined = jnp.einsum("tk,tkd->td", gate_probs, picked).astype(jnp.bfloat16)
    grad_tokens = jnp.dot(owner, returned_grad, preferred_element_type=jnp.float32).astype(
        jnp.bfloat16
    )
    return (combined, grad_tokens, grad_gate, grad_up, grad_down)


def solution(mesh):
    placed = (
        P(("expert", "replica"), None),
        P(("expert", "replica"), None),
        P(("expert", "replica"), None),
        P(("expert", "replica"), None),
        P("expert", None, None),
        P("expert", None, None),
        P("expert", None, None),
    )
    return jax.shard_map(
        per_device,
        mesh=mesh,
        in_specs=placed,
        out_specs=(
            P(("expert", "replica"), None),
            P(("expert", "replica"), None),
            P("expert", "replica", None),
            P("expert", "replica", None),
            P("expert", "replica", None),
        ),
        check_vma=False,
    )
```

```python
import jax
import jax.numpy as jnp
from jax import lax
from jax.sharding import PartitionSpec as P


def slots(routes, experts, capacity):
    flat_ids = routes.reshape(-1)
    one_hot = (flat_ids[:, None] == jnp.arange(experts, dtype=jnp.int32)[None, :]).astype(jnp.int32)
    before = jnp.cumsum(one_hot, axis=0) - one_hot
    slot_rank = jnp.sum(before * one_hot, axis=1)
    return flat_ids * capacity + slot_rank


def hidden_rows(token_rows, gate_weight, up_weight):
    pre_gate = jnp.dot(token_rows, gate_weight, preferred_element_type=jnp.float32)
    pre_up = jnp.dot(token_rows, up_weight, preferred_element_type=jnp.float32)
    activation = (jax.nn.silu(pre_gate) * pre_up).astype(jnp.bfloat16)
    return (pre_gate, pre_up, activation)


def backward_rows(grad_rows, pre_gate, pre_up, gate_weight, up_weight, down_weight):
    contract = (((1,), (1,)), ((), ()))
    d_hidden = lax.dot_general(grad_rows, down_weight, contract, preferred_element_type=jnp.float32)
    sigmoid_gate = jax.nn.sigmoid(pre_gate)
    d_gate = (d_hidden * pre_up * sigmoid_gate * (1.0 + pre_gate * (1.0 - sigmoid_gate))).astype(
        jnp.bfloat16
    )
    d_up = (d_hidden * pre_gate * sigmoid_gate).astype(jnp.bfloat16)
    back_rows = lax.dot_general(d_gate, gate_weight, contract, preferred_element_type=jnp.float32)
    back_rows = back_rows + lax.dot_general(
        d_up, up_weight, contract, preferred_element_type=jnp.float32
    )
    return (back_rows.astype(jnp.bfloat16), d_gate, d_up)


def outer_sum(left, right):
    return lax.dot_general(
        left, right, (((0,), (0,)), ((), ())), preferred_element_type=jnp.float32
    )


def exchange(blocks):
    return lax.all_to_all(blocks, "expert", split_axis=0, concat_axis=0, tiled=True)


def per_device(tokens, route_ids, gate_probs, out_cot, w_gate, w_up, w_down):
    experts = lax.axis_size("expert")
    tok_rows, features = tokens.shape
    top_count = route_ids.shape[1]
    hidden = w_gate.shape[2]
    capacity = max(2, tok_rows * top_count * 4 // (3 * experts))
    total_rows = experts * capacity
    positions = slots(route_ids, experts, capacity)
    gate_weight = w_gate[0]
    up_weight = w_up[0]
    down_weight = w_down[0]
    pick = (positions[:, None] == jnp.arange(total_rows, dtype=positions.dtype)[None, :]).astype(
        jnp.bfloat16
    )
    pick3 = pick.reshape(tok_rows, top_count, total_rows)
    owner = jnp.sum(pick3, axis=1)
    outgoing = jnp.dot(owner.T, tokens, preferred_element_type=jnp.float32).astype(jnp.bfloat16)
    slot_rows = exchange(outgoing.reshape(experts, capacity, features)).reshape(-1, features)
    scaled = (gate_probs[:, :, None] * out_cot[:, None, :].astype(jnp.float32)).astype(jnp.bfloat16)
    grad_out = jnp.dot(
        pick.T, scaled.reshape(-1, features), preferred_element_type=jnp.float32
    ).astype(jnp.bfloat16)
    grads_in = exchange(grad_out.reshape(experts, capacity, features)).reshape(-1, features)

    pre_gate, pre_up, activation = hidden_rows(slot_rows, gate_weight, up_weight)
    result = jnp.dot(activation, down_weight, preferred_element_type=jnp.float32).astype(
        jnp.bfloat16
    )
    pre_gate, pre_up, activation, result = lax.optimization_barrier(
        (pre_gate, pre_up, activation, result)
    )
    returned = exchange(result.reshape(experts, capacity, features)).reshape(-1, features)
    back_rows, d_gate, d_up = backward_rows(
        grads_in, pre_gate, pre_up, gate_weight, up_weight, down_weight
    )
    returned_grad = exchange(back_rows.reshape(experts, capacity, features)).reshape(-1, features)

    picked = jnp.einsum("tkp,pd->tkd", pick3, returned, preferred_element_type=jnp.float32)
    combined = jnp.einsum("tk,tkd->td", gate_probs, picked).astype(jnp.bfloat16)
    grad_tokens = jnp.dot(owner, returned_grad, preferred_element_type=jnp.float32).astype(
        jnp.bfloat16
    )
    gate_up_sum = lax.psum_scatter(
        jnp.einsum(
            "rd,krh->kdh",
            slot_rows,
            jnp.stack([d_gate, d_up]),
            preferred_element_type=jnp.float32,
        ).astype(jnp.bfloat16),
        "replica",
        scatter_dimension=1,
        tiled=True,
    )
    down_sum = lax.psum_scatter(
        outer_sum(activation, grads_in).astype(jnp.bfloat16),
        "replica",
        scatter_dimension=0,
        tiled=True,
    )
    grad_gate = gate_up_sum[0][None]
    grad_up = gate_up_sum[1][None]
    grad_down = down_sum[None]
    return (combined, grad_tokens, grad_gate, grad_up, grad_down)


def solution(mesh):
    placed = (
        P(("expert", "replica"), None),
        P(("expert", "replica"), None),
        P(("expert", "replica"), None),
        P(("expert", "replica"), None),
        P("expert", None, None),
        P("expert", None, None),
        P("expert", None, None),
    )
    return jax.shard_map(
        per_device,
        mesh=mesh,
        in_specs=placed,
        out_specs=(
            P(("expert", "replica"), None),
            P(("expert", "replica"), None),
            P("expert", "replica", None),
            P("expert", "replica", None),
            P("expert", "replica", None),
        ),
        check_vma=False,
    )
```

```python
import jax
import jax.numpy as jnp
from jax import lax
from jax.sharding import PartitionSpec as P


def slots(routes, experts, capacity):
    flat_ids = routes.reshape(-1)
    one_hot = (flat_ids[:, None] == jnp.arange(experts, dtype=jnp.int32)[None, :]).astype(jnp.int32)
    before = jnp.cumsum(one_hot, axis=0) - one_hot
    slot_rank = jnp.sum(before * one_hot, axis=1)
    return flat_ids * capacity + slot_rank


def hidden_rows(token_rows, gate_weight, up_weight):
    pre_gate = jnp.dot(token_rows, gate_weight, preferred_element_type=jnp.float32)
    pre_up = jnp.dot(token_rows, up_weight, preferred_element_type=jnp.float32)
    activation = (jax.nn.silu(pre_gate) * pre_up).astype(jnp.bfloat16)
    return (pre_gate, pre_up, activation)


def backward_rows(grad_rows, pre_gate, pre_up, gate_weight, up_weight, down_weight):
    contract = (((1,), (1,)), ((), ()))
    d_hidden = lax.dot_general(grad_rows, down_weight, contract, preferred_element_type=jnp.float32)
    sigmoid_gate = jax.nn.sigmoid(pre_gate)
    d_gate = (d_hidden * pre_up * sigmoid_gate * (1.0 + pre_gate * (1.0 - sigmoid_gate))).astype(
        jnp.bfloat16
    )
    d_up = (d_hidden * pre_gate * sigmoid_gate).astype(jnp.bfloat16)
    back_rows = lax.dot_general(d_gate, gate_weight, contract, preferred_element_type=jnp.float32)
    back_rows = back_rows + lax.dot_general(
        d_up, up_weight, contract, preferred_element_type=jnp.float32
    )
    return (back_rows.astype(jnp.bfloat16), d_gate, d_up)


def outer_sum(left, right):
    return lax.dot_general(
        left, right, (((0,), (0,)), ((), ())), preferred_element_type=jnp.float32
    )


def exchange(blocks):
    return lax.all_to_all(blocks, "expert", split_axis=0, concat_axis=0, tiled=True)


def per_device(tokens, route_ids, gate_probs, out_cot, w_gate, w_up, w_down):
    experts = lax.axis_size("expert")
    tok_rows, features = tokens.shape
    top_count = route_ids.shape[1]
    hidden = w_gate.shape[2]
    capacity = max(2, tok_rows * top_count * 4 // (3 * experts))
    total_rows = experts * capacity
    positions = slots(route_ids, experts, capacity)
    gate_weight = w_gate[0]
    up_weight = w_up[0]
    down_weight = w_down[0]
    pick = (positions[:, None] == jnp.arange(total_rows, dtype=positions.dtype)[None, :]).astype(
        jnp.bfloat16
    )
    pick3 = pick.reshape(tok_rows, top_count, total_rows)
    owner = jnp.sum(pick3, axis=1)
    taken = (owner > 0).astype(jnp.int32)
    source = jnp.sum(taken * jnp.arange(tok_rows, dtype=jnp.int32)[:, None], axis=0)
    source = source + tok_rows * (1 - jnp.sum(taken, axis=0))
    outgoing = jnp.take(tokens, source, axis=0, mode="fill", fill_value=0)
    slot_rows = exchange(outgoing.reshape(experts, capacity, features)).reshape(-1, features)
    scaled = (gate_probs[:, :, None] * out_cot[:, None, :].astype(jnp.float32)).astype(jnp.bfloat16)
    grad_out = jnp.dot(
        pick.T, scaled.reshape(-1, features), preferred_element_type=jnp.float32
    ).astype(jnp.bfloat16)
    grads_in = exchange(grad_out.reshape(experts, capacity, features)).reshape(-1, features)

    pre_gate, pre_up, activation = hidden_rows(slot_rows, gate_weight, up_weight)
    result = jnp.dot(activation, down_weight, preferred_element_type=jnp.float32).astype(
        jnp.bfloat16
    )
    pre_gate, pre_up, activation, result = lax.optimization_barrier(
        (pre_gate, pre_up, activation, result)
    )
    returned = exchange(result.reshape(experts, capacity, features)).reshape(-1, features)
    back_rows, d_gate, d_up = backward_rows(
        grads_in, pre_gate, pre_up, gate_weight, up_weight, down_weight
    )
    returned_grad = exchange(back_rows.reshape(experts, capacity, features)).reshape(-1, features)

    picked = jnp.einsum("tkp,pd->tkd", pick3, returned, preferred_element_type=jnp.float32)
    combined = jnp.einsum("tk,tkd->td", gate_probs, picked).astype(jnp.bfloat16)
    grad_tokens = jnp.dot(owner, returned_grad, preferred_element_type=jnp.float32).astype(
        jnp.bfloat16
    )
    gate_up_grad = jnp.concatenate([d_gate, d_up], axis=1)
    gate_up_sum = lax.psum_scatter(
        outer_sum(slot_rows, gate_up_grad).astype(jnp.bfloat16),
        "replica",
        scatter_dimension=0,
        tiled=True,
    ).astype(jnp.float32)
    down_sum = lax.psum_scatter(
        outer_sum(activation, grads_in).astype(jnp.bfloat16),
        "replica",
        scatter_dimension=0,
        tiled=True,
    )
    grad_gate = gate_up_sum[:, :hidden].astype(jnp.bfloat16)[None]
    grad_up = gate_up_sum[:, hidden:].astype(jnp.bfloat16)[None]
    grad_down = down_sum[None]
    return (combined, grad_tokens, grad_gate, grad_up, grad_down)


def solution(mesh):
    placed = (
        P(("expert", "replica"), None),
        P(("expert", "replica"), None),
        P(("expert", "replica"), None),
        P(("expert", "replica"), None),
        P("expert", None, None),
        P("expert", None, None),
        P("expert", None, None),
    )
    return jax.shard_map(
        per_device,
        mesh=mesh,
        in_specs=placed,
        out_specs=(
            P(("expert", "replica"), None),
            P(("expert", "replica"), None),
            P("expert", "replica", None),
            P("expert", "replica", None),
            P("expert", "replica", None),
        ),
        check_vma=False,
    )
```

```python
import jax
import jax.numpy as jnp
from jax import lax
from jax.sharding import PartitionSpec as P


def slots(routes, experts, capacity):
    flat_ids = routes.reshape(-1)
    one_hot = (flat_ids[:, None] == jnp.arange(experts, dtype=jnp.int32)[None, :]).astype(jnp.int32)
    rows = flat_ids.shape[0]
    lower = jnp.arange(rows)[:, None] > jnp.arange(rows)[None, :]
    before = jnp.dot(
        lower.astype(jnp.bfloat16), one_hot.astype(jnp.bfloat16), preferred_element_type=jnp.float32
    ).astype(jnp.int32)
    slot_rank = jnp.sum(before * one_hot, axis=1)
    return flat_ids * capacity + slot_rank


def hidden_rows(token_rows, gate_weight, up_weight):
    pre_gate = jnp.dot(token_rows, gate_weight, preferred_element_type=jnp.float32)
    pre_up = jnp.dot(token_rows, up_weight, preferred_element_type=jnp.float32)
    activation = (jax.nn.silu(pre_gate) * pre_up).astype(jnp.bfloat16)
    return (pre_gate, pre_up, activation)


def backward_rows(grad_rows, pre_gate, pre_up, gate_weight, up_weight, down_weight):
    contract = (((1,), (1,)), ((), ()))
    d_hidden = lax.dot_general(grad_rows, down_weight, contract, preferred_element_type=jnp.float32)
    sigmoid_gate = jax.nn.sigmoid(pre_gate)
    d_gate = (d_hidden * pre_up * sigmoid_gate * (1.0 + pre_gate * (1.0 - sigmoid_gate))).astype(
        jnp.bfloat16
    )
    d_up = (d_hidden * pre_gate * sigmoid_gate).astype(jnp.bfloat16)
    back_rows = lax.dot_general(d_gate, gate_weight, contract, preferred_element_type=jnp.float32)
    back_rows = back_rows + lax.dot_general(
        d_up, up_weight, contract, preferred_element_type=jnp.float32
    )
    return (back_rows.astype(jnp.bfloat16), d_gate, d_up)


def outer_sum(left, right):
    return lax.dot_general(
        left, right, (((0,), (0,)), ((), ())), preferred_element_type=jnp.float32
    )


def exchange(blocks):
    return lax.all_to_all(blocks, "expert", split_axis=0, concat_axis=0, tiled=True)


def per_device(tokens, route_ids, gate_probs, out_cot, w_gate, w_up, w_down):
    experts = lax.axis_size("expert")
    tok_rows, features = tokens.shape
    top_count = route_ids.shape[1]
    hidden = w_gate.shape[2]
    capacity = max(2, tok_rows * top_count * 4 // (3 * experts))
    total_rows = experts * capacity
    positions = slots(route_ids, experts, capacity)
    gate_weight = w_gate[0]
    up_weight = w_up[0]
    down_weight = w_down[0]
    pick = (positions[:, None] == jnp.arange(total_rows, dtype=positions.dtype)[None, :]).astype(
        jnp.bfloat16
    )
    pick3 = pick.reshape(tok_rows, top_count, total_rows)
    owner = jnp.sum(pick3, axis=1)
    outgoing = jnp.dot(owner.T, tokens, preferred_element_type=jnp.float32).astype(jnp.bfloat16)
    slot_rows = exchange(outgoing.reshape(experts, capacity, features)).reshape(-1, features)
    scaled = (gate_probs[:, :, None] * out_cot[:, None, :].astype(jnp.float32)).astype(jnp.bfloat16)
    grad_out = jnp.dot(
        pick.T, scaled.reshape(-1, features), preferred_element_type=jnp.float32
    ).astype(jnp.bfloat16)
    grads_in = exchange(grad_out.reshape(experts, capacity, features)).reshape(-1, features)

    pre_gate, pre_up, activation = hidden_rows(slot_rows, gate_weight, up_weight)
    result = jnp.dot(activation, down_weight, preferred_element_type=jnp.float32).astype(
        jnp.bfloat16
    )
    pre_gate, pre_up, activation, result = lax.optimization_barrier(
        (pre_gate, pre_up, activation, result)
    )
    returned = exchange(result.reshape(experts, capacity, features)).reshape(-1, features)
    back_rows, d_gate, d_up = backward_rows(
        grads_in, pre_gate, pre_up, gate_weight, up_weight, down_weight
    )
    returned_grad = exchange(back_rows.reshape(experts, capacity, features)).reshape(-1, features)

    picked = jnp.einsum("tkp,pd->tkd", pick3, returned, preferred_element_type=jnp.float32)
    combined = jnp.einsum("tk,tkd->td", gate_probs, picked).astype(jnp.bfloat16)
    grad_tokens = jnp.dot(owner, returned_grad, preferred_element_type=jnp.float32).astype(
        jnp.bfloat16
    )
    gate_up_grad = jnp.concatenate([d_gate, d_up], axis=1)
    gate_up_sum = lax.psum_scatter(
        outer_sum(slot_rows, gate_up_grad).astype(jnp.bfloat16),
        "replica",
        scatter_dimension=0,
        tiled=True,
    ).astype(jnp.float32)
    down_sum = lax.psum_scatter(
        outer_sum(activation, grads_in).astype(jnp.bfloat16),
        "replica",
        scatter_dimension=0,
        tiled=True,
    )
    grad_gate = gate_up_sum[:, :hidden].astype(jnp.bfloat16)[None]
    grad_up = gate_up_sum[:, hidden:].astype(jnp.bfloat16)[None]
    grad_down = down_sum[None]
    return (combined, grad_tokens, grad_gate, grad_up, grad_down)


def solution(mesh):
    placed = (
        P(("expert", "replica"), None),
        P(("expert", "replica"), None),
        P(("expert", "replica"), None),
        P(("expert", "replica"), None),
        P("expert", None, None),
        P("expert", None, None),
        P("expert", None, None),
    )
    return jax.shard_map(
        per_device,
        mesh=mesh,
        in_specs=placed,
        out_specs=(
            P(("expert", "replica"), None),
            P(("expert", "replica"), None),
            P("expert", "replica", None),
            P("expert", "replica", None),
            P("expert", "replica", None),
        ),
        check_vma=False,
    )
```

```python
import jax
import jax.numpy as jnp
from jax import lax
from jax.sharding import PartitionSpec as P


def slots(routes, experts, capacity):
    flat_ids = routes.reshape(-1)
    one_hot = (flat_ids[:, None] == jnp.arange(experts, dtype=jnp.int32)[None, :]).astype(jnp.int32)
    rows = flat_ids.shape[0]
    lower = jnp.arange(rows)[:, None] > jnp.arange(rows)[None, :]
    before = jnp.dot(
        lower.astype(jnp.bfloat16), one_hot.astype(jnp.bfloat16), preferred_element_type=jnp.float32
    ).astype(jnp.int32)
    slot_rank = jnp.sum(before * one_hot, axis=1)
    return flat_ids * capacity + slot_rank


def hidden_rows(token_rows, gate_weight, up_weight):
    pre_gate = jnp.dot(token_rows, gate_weight, preferred_element_type=jnp.float32)
    pre_up = jnp.dot(token_rows, up_weight, preferred_element_type=jnp.float32)
    activation = (jax.nn.silu(pre_gate) * pre_up).astype(jnp.bfloat16)
    return (pre_gate, pre_up, activation)


def backward_rows(grad_rows, pre_gate, pre_up, gate_weight, up_weight, down_weight):
    contract = (((1,), (1,)), ((), ()))
    d_hidden = lax.dot_general(grad_rows, down_weight, contract, preferred_element_type=jnp.float32)
    sigmoid_gate = jax.nn.sigmoid(pre_gate)
    d_gate = (d_hidden * pre_up * sigmoid_gate * (1.0 + pre_gate * (1.0 - sigmoid_gate))).astype(
        jnp.bfloat16
    )
    d_up = (d_hidden * pre_gate * sigmoid_gate).astype(jnp.bfloat16)
    back_rows = lax.dot_general(d_gate, gate_weight, contract, preferred_element_type=jnp.float32)
    back_rows = back_rows + lax.dot_general(
        d_up, up_weight, contract, preferred_element_type=jnp.float32
    )
    return (back_rows.astype(jnp.bfloat16), d_gate, d_up)


def outer_sum(left, right):
    return lax.dot_general(
        left, right, (((0,), (0,)), ((), ())), preferred_element_type=jnp.float32
    )


def exchange(blocks):
    return lax.all_to_all(blocks, "expert", split_axis=0, concat_axis=0, tiled=True)


def per_device(tokens, route_ids, gate_probs, out_cot, w_gate, w_up, w_down):
    experts = lax.axis_size("expert")
    tok_rows, features = tokens.shape
    top_count = route_ids.shape[1]
    hidden = w_gate.shape[2]
    capacity = max(2, tok_rows * top_count * 4 // (3 * experts))
    total_rows = experts * capacity
    positions = slots(route_ids, experts, capacity)
    gate_weight = w_gate[0]
    up_weight = w_up[0]
    down_weight = w_down[0]
    pick = (positions[:, None] == jnp.arange(total_rows, dtype=positions.dtype)[None, :]).astype(
        jnp.bfloat16
    )
    pick3 = pick.reshape(tok_rows, top_count, total_rows)
    owner = jnp.sum(pick3, axis=1)
    slot_owner = jnp.sum(
        jnp.arange(total_rows, dtype=positions.dtype)[:, None, None]
        == positions.reshape(1, tok_rows, top_count),
        axis=2,
    ).astype(jnp.bfloat16)
    outgoing = jnp.dot(slot_owner, tokens, preferred_element_type=jnp.float32).astype(jnp.bfloat16)
    slot_rows = exchange(outgoing.reshape(experts, capacity, features)).reshape(-1, features)
    scaled = (gate_probs[:, :, None] * out_cot[:, None, :].astype(jnp.float32)).astype(jnp.bfloat16)
    grad_out = jnp.dot(
        pick.T, scaled.reshape(-1, features), preferred_element_type=jnp.float32
    ).astype(jnp.bfloat16)
    grads_in = exchange(grad_out.reshape(experts, capacity, features)).reshape(-1, features)

    pre_gate, pre_up, activation = hidden_rows(slot_rows, gate_weight, up_weight)
    result = jnp.dot(activation, down_weight, preferred_element_type=jnp.float32).astype(
        jnp.bfloat16
    )
    pre_gate, pre_up, activation, result = lax.optimization_barrier(
        (pre_gate, pre_up, activation, result)
    )
    returned = exchange(result.reshape(experts, capacity, features)).reshape(-1, features)
    back_rows, d_gate, d_up = backward_rows(
        grads_in, pre_gate, pre_up, gate_weight, up_weight, down_weight
    )
    returned_grad = exchange(back_rows.reshape(experts, capacity, features)).reshape(-1, features)

    picked = jnp.einsum("tkp,pd->tkd", pick3, returned, preferred_element_type=jnp.float32)
    combined = jnp.einsum("tk,tkd->td", gate_probs, picked).astype(jnp.bfloat16)
    grad_tokens = jnp.dot(owner, returned_grad, preferred_element_type=jnp.float32).astype(
        jnp.bfloat16
    )
    gate_up_grad = jnp.concatenate([d_gate, d_up], axis=1)
    gate_up_sum = lax.psum_scatter(
        outer_sum(slot_rows, gate_up_grad).astype(jnp.bfloat16),
        "replica",
        scatter_dimension=0,
        tiled=True,
    ).astype(jnp.float32)
    down_sum = lax.psum_scatter(
        outer_sum(activation, grads_in).astype(jnp.bfloat16),
        "replica",
        scatter_dimension=0,
        tiled=True,
    )
    grad_gate = gate_up_sum[:, :hidden].astype(jnp.bfloat16)[None]
    grad_up = gate_up_sum[:, hidden:].astype(jnp.bfloat16)[None]
    grad_down = down_sum[None]
    return (combined, grad_tokens, grad_gate, grad_up, grad_down)


def solution(mesh):
    placed = (
        P(("expert", "replica"), None),
        P(("expert", "replica"), None),
        P(("expert", "replica"), None),
        P(("expert", "replica"), None),
        P("expert", None, None),
        P("expert", None, None),
        P("expert", None, None),
    )
    return jax.shard_map(
        per_device,
        mesh=mesh,
        in_specs=placed,
        out_specs=(
            P(("expert", "replica"), None),
            P(("expert", "replica"), None),
            P("expert", "replica", None),
            P("expert", "replica", None),
            P("expert", "replica", None),
        ),
        check_vma=False,
    )
```
